32 devices in a mesh: groups: 2 (over x), space: 16 (over z, y, core).
Axes of the slice: x: 2, y: 2, z: 4, core: 2. Of those that a mesh axis runs over, the one named last changes fastest.
Arguments:
- volume: bfloat16 [64, 64, 32, 64], P(('groups', 'space')), parts along dimension 0, may hold values from -6 to 6
- weight_one: bfloat16 [3, 3, 3, 64, 64], replicated, may hold values from -0.15625 to 0.15625
- weight_two: bfloat16 [3, 3, 3, 64, 128], replicated, may hold values from -0.15625 to 0.15625
- cotangent: bfloat16 [64, 64, 32, 128], P(('groups', 'space')), parts along dimension 0, may hold values from -6 to 6
Outputs:
- output: float32 [64, 64, 32, 128], P(('groups', 'space')), parts along dimension 0
- grad_volume: float32 [64, 64, 32, 64], P(('groups', 'space')), parts along dimension 0
- grad_one: float32 [6, 3, 3, 64, 64], P('groups', None, None, None, 'space'), parts along dimension 0
- grad_two: float32 [6, 3, 3, 64, 128], P('groups', None, None, None, 'space'), parts along dimension 0
The draws below stay inside these ranges and needn't reach their ends.
There are 2 independent parts, one for each index of `groups`. The reference program is written for one: setup_inputs(seed, part) draws one part's arguments, and reference() takes and returns one part's arrays. A program takes and returns all parts, laid end to end along the dimension named above; an argument that names none is the same for every part. Nothing has to cross between parts.
All inputs are finite; a program needn't handle non-finite values.
Results may differ from the reference program's by a relative error of at most 0.0029.
Values may be sent and summed in bfloat16 or wider, within the bound.
A program may use at most 64 MiB of HBM per device.

```python
import math
import jax
import jax.numpy as jnp
from jax import lax

CH_IN = 64
CH_MID = 64
CH_OUT = 128
HEIGHT = 64
WIDTH = 32
DEPTH = 32
CELLS = 65536


def raised(result, own_key, source, target, parts, factor):
    owner, partner = [(jnp.arange(result.shape[dim]) // (result.shape[dim] // parts)).reshape([-1 if axis == dim else 1 for axis in range(result.ndim)]) for dim in (source, target)]
    chosen = jax.random.permutation(own_key, parts)[partner]
    strong = (owner == chosen) | (owner == (partner + parts // 2) % parts)
    return jnp.where(strong, factor * result, result)


def block_levels(key, extent, cuts, smallest, top_value):
    def one(axis_at, blocks):
        heights = jax.random.uniform(jax.random.fold_in(jax.random.fold_in(key, 6), axis_at), (blocks,), jnp.float32, smallest / len(cuts), top_value / len(cuts))
        return jnp.repeat(jnp.exp(heights), extent[axis_at] // blocks).reshape((-1,) + (1,) * (len(extent) - axis_at - 1))

    loudness = one(*cuts[0])
    for cut in cuts[1:]:
        loudness = loudness * one(*cut)
    return loudness


def scatter_about(key, extent, spread, limit, cuts=(), kind=jnp.bfloat16):
    array = spread * jax.random.normal(key, extent, jnp.float32)
    if cuts:
        array = array * block_levels(key, extent, cuts, -0.22, 0.18)
    return jnp.clip(array, -limit, limit).astype(kind)


def gaussian_with(rng, shape, scale, reach, cuts, heavy, kind=jnp.bfloat16):
    values = scale * jax.random.normal(rng, shape, jnp.float32)
    if cuts:
        values = values * block_levels(rng, shape, cuts, -0.22, 0.18)
    return jnp.clip(raised(values, jax.random.fold_in(rng, 3), *heavy), -reach, reach).astype(kind)


def setup_inputs(seed: int = 0, part: int = 0) -> dict:
    key_of = jax.random.split(jax.random.key(seed), 5)
    part_keys = jax.random.split(jax.random.fold_in(key_of[4], part), 5)
    volume = scatter_about(part_keys[0], (DEPTH, HEIGHT, WIDTH, CH_IN), 1.0, 6.0, ((0, 16),))
    weight_one = scatter_about(key_of[1], (3, 3, 3, CH_IN, CH_MID), (27 * CH_IN) ** -0.5, 0.15625)
    weight_two = scatter_about(key_of[2], (3, 3, 3, CH_MID, CH_OUT), (27 * CH_MID) ** -0.5, 0.15625)
    cotangent = gaussian_with(part_keys[3], (DEPTH, HEIGHT, WIDTH, CH_OUT), 1.0, 6.0, ((0, 16),), (0, 3, 16, 2.0))
    return dict(volume=volume, weight_one=weight_one, weight_two=weight_two, cotangent=cotangent)


def pad_cells(field):
    return jnp.pad(field, ((1, 1), (1, 1), (1, 1), (0, 0)))

def conv_valid(padded, kernel):
    return lax.conv_general_dilated(padded[None], kernel, (1, 1, 1), 'VALID', dimension_numbers=('NDHWC', 'DHWIO', 'NDHWC'), precision=lax.Precision.HIGHEST)[0]

def flipped(kernel):
    return jnp.transpose(kernel[::-1, ::-1, ::-1], (0, 1, 2, 4, 3))

def kernel_terms(padded, grad_field):
    depth_len, rows_len, cols_len = (grad_field.shape[0], grad_field.shape[1], grad_field.shape[2])
    flat_grad = grad_field.reshape(-1, grad_field.shape[3])
    results = []
    for depth_tap in range(3):
        for row_tap in range(3):
            for column_tap in range(3):
                window = padded[depth_tap:depth_tap + depth_len, row_tap:row_tap + rows_len, column_tap:column_tap + cols_len]
                results.append(lax.dot_general(window.reshape(-1, padded.shape[3]), flat_grad, (((0,), (0,)), ((), ())), precision=lax.Precision.HIGHEST))
    return jnp.stack(results).reshape(3, 3, 3, padded.shape[3], grad_field.shape[3])

def reference(volume, weight_one, weight_two, cotangent):
    inputs = volume.astype(jnp.float32)
    kernel_one = weight_one.astype(jnp.float32)
    kernel_two = weight_two.astype(jnp.float32)
    grad_out = cotangent.astype(jnp.float32)
    hidden = conv_valid(pad_cells(inputs), kernel_one)
    sigmoid_hidden = jax.nn.sigmoid(hidden)
    activation = (hidden * sigmoid_hidden).astype(jnp.bfloat16).astype(jnp.float32)
    output = conv_valid(pad_cells(activation), kernel_two)
    grad_act = conv_valid(pad_cells(grad_out), flipped(kernel_two))
    grad_hidden = (grad_act * sigmoid_hidden * (1.0 + hidden * (1.0 - sigmoid_hidden))).astype(jnp.bfloat16).astype(jnp.float32)
    grad_volume = conv_valid(pad_cells(grad_hidden), flipped(kernel_one))
    scale = 1.0 / math.sqrt(CELLS)
    grad_one = kernel_terms(pad_cells(inputs), grad_hidden) * scale
    grad_two = kernel_terms(pad_cells(activation), grad_out) * scale
    return (output, grad_volume, grad_one, grad_two)
```

```python
import functools
import math

import jax
import jax.numpy as jnp
from jax import lax
from jax.experimental import pallas as pl
from jax.experimental.pallas import tpu as pltpu
from jax.sharding import PartitionSpec as P

MESH = pl.DeviceIdType.MESH
F32 = jnp.float32
BF16 = jnp.bfloat16
TN = (((0,), (0,)), ((), ()))


def kernel(
    n, planes, height, width, ci, cm, co, scale,
    vol, cot, w1, w2, w1f, wg,
    out, gvol, g1, g2,
    pv, pa, pg, ct, vraw, araw, graw, vh, ah, gh, dsl, acc1, acc2, tx, rx,
    loc_sem, hs_sem, hr_sem, ts_sem, tr_sem,
):
    me = lax.axis_index("space")
    plane = height * width
    chunk = plane // 4
    pad = plane + 2 * width
    r1, r2 = cm // n, co // n

    barrier = pltpu.get_barrier_semaphore()
    for j in range(1, n):
        pl.semaphore_signal(
            barrier, inc=1, device_id={"space": lax.rem(me + j, n)}, device_id_type=MESH
        )

    local = [pltpu.make_async_copy(vol, vraw, loc_sem.at[0])]
    for p in range(planes):
        local.append(
            pltpu.make_async_copy(
                cot.at[pl.ds(p * plane, plane)],
                ct.at[p + 1, pl.ds(width, plane)],
                loc_sem.at[1 + p],
            )
        )
    for copy in local:
        copy.start()

    for ref in (pv, pa, pg, ct):
        zero = jnp.zeros((width, ref.shape[2]), BF16)
        for p in range(planes + 2):
            ref[p, pl.ds(0, width), :] = zero
            ref[p, pl.ds(pad - width, width), :] = zero

    column = lax.broadcasted_iota(jnp.int32, (chunk, 1), 0) % width
    first = column == 0
    last = column == width - 1

    def spread(x, ref, p, row):
        back = jnp.where(first, 0.0, pltpu.roll(x, 1, 0))
        ahead = jnp.where(last, 0.0, pltpu.roll(x, chunk - 1, 0))
        ref[p, pl.ds(row, chunk), :] = jnp.concatenate([back, x, ahead], axis=1).astype(BF16)

    def each(count, body):
        def step(k, carry):
            body(k // 4, pl.multiple_of(lax.rem(k, 4) * chunk, chunk))
            return carry

        lax.fori_loop(0, 4 * count, step, 0)

    def halo(kind, low_src, high_src, low_dst, high_dst):
        left = pltpu.make_async_remote_copy(
            low_src, high_dst, hs_sem.at[kind, 0], hr_sem.at[kind, 0],
            device_id={"space": lax.rem(me + n - 1, n)}, device_id_type=MESH,
        )
        right = pltpu.make_async_remote_copy(
            high_src, low_dst, hs_sem.at[kind, 1], hr_sem.at[kind, 1],
            device_id={"space": lax.rem(me + 1, n)}, device_id_type=MESH,
        )

        def start():
            @pl.when(me > 0)
            def _():
                left.start()

            @pl.when(me < n - 1)
            def _():
                right.start()

        def wait_recv():
            @pl.when(me < n - 1)
            def _():
                left.wait_recv()

            @pl.when(me == n - 1)
            def _():
                high_dst[...] = jnp.zeros(high_dst.shape, BF16)

            @pl.when(me > 0)
            def _():
                right.wait_recv()

            @pl.when(me == 0)
            def _():
                low_dst[...] = jnp.zeros(low_dst.shape, BF16)

        def wait_send():
            @pl.when(me > 0)
            def _():
                left.wait_send()

            @pl.when(me < n - 1)
            def _():
                right.wait_send()

        return start, wait_recv, wait_send

    end = (planes - 1) * plane
    volume_halo = halo(
        0, vol.at[pl.ds(0, plane)], vol.at[pl.ds(end, plane)], vh.at[0], vh.at[1]
    )
    cot_halo = halo(
        1, cot.at[pl.ds(0, plane)], cot.at[pl.ds(end, plane)],
        ct.at[0, pl.ds(width, plane)], ct.at[planes + 1, pl.ds(width, plane)],
    )
    act_halo = halo(
        2, araw.at[pl.ds(0, plane)], araw.at[pl.ds(end, plane)], ah.at[0], ah.at[1]
    )
    grad_halo = halo(
        3, graw.at[pl.ds(0, plane)], graw.at[pl.ds(end, plane)], gh.at[0], gh.at[1]
    )

    pl.semaphore_wait(barrier, n - 1)
    volume_halo[0]()
    cot_halo[0]()

    local[0].wait()

    def own_volume(p, row):
        x = vraw[pl.ds(pl.multiple_of(p * plane + row, chunk), chunk), :].astype(F32)
        spread(x, pv, p + 1, row + width)

    each(planes, own_volume)

    def halo_planes(slots, ref):
        def body(p, row):
            x = slots[p, pl.ds(row, chunk), :].astype(F32)
            spread(x, ref, p * (planes + 1), row + width)

        each(2, body)

    def conv(ref, kernels, p, row):
        total = None
        for a in range(3):
            for b in range(3):
                term = jnp.dot(
                    ref[p + a, pl.ds(pl.multiple_of(row + b * width, width), chunk), :],
                    kernels[a * 3 + b],
                    preferred_element_type=F32,
                )
                total = term if total is None else total + term
        return total

    volume_halo[1]()
    halo_planes(vh, pv)

    def first_conv(p, row):
        hidden = conv(pv, w1, p, row)
        s = jax.nn.sigmoid(hidden)
        at = pl.ds(pl.multiple_of(p * plane + row, chunk), chunk)
        dsl[at, :] = s * (1.0 + hidden * (1.0 - s))
        rounded = (hidden * s).astype(BF16)
        araw[at, :] = rounded
        spread(rounded.astype(F32), pa, p + 1, row + width)

    each(planes, first_conv)
    act_halo[0]()

    for copy in local[1:]:
        copy.wait()
    cot_halo[1]()
    low_lanes = lax.broadcasted_iota(jnp.int32, (1, 2 * cm), 1) < cm

    def back_conv(p, row):
        pieces = [
            ct[p + a, pl.ds(pl.multiple_of(row + b * width, width), chunk), :]
            for a in range(3)
            for b in range(3)
        ]
        y = jnp.dot(jnp.concatenate(pieces, axis=1), wg[...], preferred_element_type=F32)
        z = y[:, : 2 * cm]
        z = jnp.where(
            low_lanes,
            jnp.where(first, 0.0, pltpu.roll(z, 1, 0)),
            jnp.where(last, 0.0, pltpu.roll(z, chunk - 1, 0)),
        )
        grad_act = z[:, :cm] + z[:, cm:] + y[:, 2 * cm :]
        at = pl.ds(pl.multiple_of(p * plane + row, chunk), chunk)
        rounded = (grad_act * dsl[at, :]).astype(BF16)
        graw[at, :] = rounded
        spread(rounded.astype(F32), pg, p + 1, row + width)

    each(planes, back_conv)
    grad_halo[0]()

    act_halo[1]()
    halo_planes(ah, pa)

    acc1[...] = jnp.zeros(acc1.shape, F32)
    acc2[...] = jnp.zeros(acc2.shape, F32)

    def kernel_terms(p, row):
        at = pl.ds(pl.multiple_of(p * plane + row, chunk), chunk)
        field2 = ct[p + 1, pl.ds(pl.multiple_of(row + width, width), chunk), :].T
        field1 = graw[at, :].T
        for a in range(3):
            for b in range(3):
                rows = pl.ds(pl.multiple_of(row + b * width, width), chunk)
                acc2[a * 3 + b] += jnp.dot(field2, pa[p + a, rows, :], preferred_element_type=F32)
                acc1[a * 3 + b] += jnp.dot(field1, pv[p + a, rows, :], preferred_element_type=F32)

    each(planes, kernel_terms)

    blank = jnp.zeros((tx.shape[2] - r1 - r2, 3 * ci), F32)
    for t in range(9):
        for s in range(n):
            tile = jnp.concatenate(
                [
                    acc2[t, pl.ds(s * r2, r2), :],
                    acc1[t, pl.ds(s * r1, r1), :],
                    blank,
                ],
                axis=0,
            ).astype(BF16)
            tx[s, t] = tile[:, : 2 * ci]
            tx[s, 9 + t // 2, :, pl.ds((t % 2) * ci, ci)] = tile[:, 2 * ci :]
    for s in range(n):
        tx[s, 13, :, pl.ds(ci, ci)] = jnp.zeros((tx.shape[2], ci), BF16)

    sends = []
    for j in range(1, n):
        owner = lax.rem(me + j, n)
        sends.append(
            pltpu.make_async_remote_copy(
                tx.at[owner], rx.at[j], ts_sem.at[j], tr_sem.at[j],
                device_id={"space": owner}, device_id_type=MESH,
            )
        )
        sends[-1].start()

    def second_conv(p, row):
        at = pl.ds(pl.multiple_of(p * plane + row, chunk), chunk)
        out[at, :] = conv(pa, w2, p, row)

    each(planes, second_conv)

    grad_halo[1]()
    halo_planes(gh, pg)

    def last_conv(p, row):
        at = pl.ds(pl.multiple_of(p * plane + row, chunk), chunk)
        gvol[at, :] = conv(pg, w1f, p, row)

    each(planes, last_conv)

    for send in sends:
        send.wait_recv()
    for t in range(14):
        total = tx[me, t].astype(F32)
        for j in range(1, n):
            total = total + rx[j, t].astype(F32)
        total = total * scale
        taps = (3 * t, 3 * t + 1) if t < 9 else (3 * (2 * (t - 9)) + 2, 3 * (2 * (t - 9) + 1) + 2)
        for half, tap in enumerate(taps):
            if tap < 27:
                part = total[:, half * ci : (half + 1) * ci]
                g2[tap] = part[:r2]
                g1[tap] = part[r2 : r2 + r1]

    for send in sends:
        send.wait_send()
    for exchange in (volume_halo, cot_halo, act_halo, grad_halo):
        exchange[2]()


def shards(volume, weight_one, weight_two, cotangent):
    n = lax.axis_size("space")
    planes, height, width, ci = volume.shape
    cm, co = weight_two.shape[3], weight_two.shape[4]
    plane = height * width
    cells = planes * plane
    pad = plane + 2 * width
    scale = 1.0 / math.sqrt(cells * n)

    w1 = weight_one.reshape(9, 3 * ci, cm)
    w2 = weight_two.reshape(9, 3 * cm, co)
    w1f = jnp.transpose(weight_one[::-1, ::-1, ::-1], (0, 1, 2, 4, 3)).reshape(9, 3 * cm, ci)
    wg = jnp.transpose(weight_two[::-1, ::-1, ::-1], (0, 1, 4, 2, 3))
    wg = jnp.concatenate([wg[:, :, :, 0], wg[:, :, :, 2], wg[:, :, :, 1]], axis=3)
    wg = wg.reshape(9 * co, 3 * cm)

    vmem = pl.BlockSpec(memory_space=pltpu.VMEM)
    hbm = pl.BlockSpec(memory_space=pl.ANY)
    rows = -(-(cm // n + co // n) // 16) * 16
    out, gvol, g1, g2 = pl.pallas_call(
        functools.partial(kernel, n, planes, height, width, ci, cm, co, scale),
        out_shape=(
            jax.ShapeDtypeStruct((cells, co), F32),
            jax.ShapeDtypeStruct((cells, ci), F32),
            jax.ShapeDtypeStruct((27, cm // n, ci), F32),
            jax.ShapeDtypeStruct((27, co // n, cm), F32),
        ),
        in_specs=[hbm, hbm, vmem, vmem, vmem, vmem],
        out_specs=(vmem, vmem, vmem, vmem),
        scratch_shapes=[
            pltpu.VMEM((planes + 2, pad, 3 * ci), BF16),
            pltpu.VMEM((planes + 2, pad, 3 * cm), BF16),
            pltpu.VMEM((planes + 2, pad, 3 * cm), BF16),
            pltpu.VMEM((planes + 2, pad, co), BF16),
            pltpu.VMEM((cells, ci), BF16),
            pltpu.VMEM((cells, cm), BF16),
            pltpu.VMEM((cells, cm), BF16),
            pltpu.VMEM((2, plane, ci), BF16),
            pltpu.VMEM((2, plane, cm), BF16),
            pltpu.VMEM((2, plane, cm), BF16),
            pltpu.VMEM((cells, cm), F32),
            pltpu.VMEM((9, cm, 3 * ci), F32),
            pltpu.VMEM((9, co, 3 * cm), F32),
            pltpu.VMEM((n, 14, rows, 2 * ci), BF16),
            pltpu.VMEM((n, 14, rows, 2 * ci), BF16),
            pltpu.SemaphoreType.DMA((1 + planes,)),
            pltpu.SemaphoreType.DMA((4, 2)),
            pltpu.SemaphoreType.DMA((4, 2)),
            pltpu.SemaphoreType.DMA((n,)),
            pltpu.SemaphoreType.DMA((n,)),
        ],
        compiler_params=pltpu.CompilerParams(
            collective_id=0, has_side_effects=True, vmem_limit_bytes=60 << 20
        ),
    )(
        volume.reshape(cells, ci), cotangent.reshape(cells, co), w1, w2, w1f, wg
    )
    return (
        out.reshape(planes, height, width, co),
        gvol.reshape(planes, height, width, ci),
        jnp.transpose(g1.reshape(3, 3, 3, cm // n, ci), (0, 1, 2, 4, 3)),
        jnp.transpose(g2.reshape(3, 3, 3, co // n, cm), (0, 1, 2, 4, 3)),
    )


def solution(mesh):
    return jax.shard_map(
        shards,
        mesh=mesh,
        in_specs=(
            P(("groups", "space"), None, None, None),
            P(),
            P(),
            P(("groups", "space"), None, None, None),
        ),
        out_specs=(
            P(("groups", "space"), None, None, None),
            P(("groups", "space"), None, None, None),
            P("groups", None, None, None, "space"),
            P("groups", None, None, None, "space"),
        ),
        check_vma=False,
    )
```

```python
import functools
import math

import jax
import jax.numpy as jnp
from jax import lax
from jax.experimental import pallas as pl
from jax.experimental.pallas import tpu as pltpu
from jax.sharding import PartitionSpec as P

MESH = pl.DeviceIdType.MESH
F32 = jnp.float32
BF16 = jnp.bfloat16
TN = (((0,), (0,)), ((), ()))


def kernel(
    n, planes, height, width, ci, cm, co, scale,
    vol, cot, w1, w2,
    out, gvol, g1, g2,
    pv, pa, pg, ct, vraw, araw, graw, vs, sa, gs, vh, ah, gh, dsl, acc1, acc2,
    w1f, wg, own, tx, rx, ty, ry,
    loc_sem, hs_sem, hr_sem, ps_sem, pr_sem, ts_sem, tr_sem,
):
    me = lax.axis_index("space")
    plane = height * width
    chunk = plane // 4
    pad = plane + 2 * width
    r1, r2 = cm // n, co // n

    barrier = pltpu.get_barrier_semaphore()
    for j in range(1, n):
        pl.semaphore_signal(
            barrier, inc=1, device_id={"space": lax.rem(me + j, n)}, device_id_type=MESH
        )

    local = [pltpu.make_async_copy(vol, vraw, loc_sem.at[0])]
    for p in range(planes):
        local.append(
            pltpu.make_async_copy(
                cot.at[pl.ds(p * plane, plane)],
                ct.at[p + 1, pl.ds(width, plane)],
                loc_sem.at[1 + p],
            )
        )
    for copy in local:
        copy.start()

    for t in range(9):
        w = w2[8 - t]
        order = [w[2 * cm :], w[:cm], w[cm : 2 * cm]]
        wg[pl.ds(t * co, co), :] = jnp.concatenate(order, axis=0).T
        w = w1[8 - t]
        for c in range(3):
            w1f[t, pl.ds(c * cm, cm), :] = w[(2 - c) * ci : (3 - c) * ci].T

    for ref in (pv, pa, pg, ct):
        zero = jnp.zeros((width, ref.shape[2]), BF16)
        for p in range(planes + 2):
            ref[p, pl.ds(0, width), :] = zero
            ref[p, pl.ds(pad - width, width), :] = zero

    column = lax.broadcasted_iota(jnp.int32, (chunk, 1), 0) % width
    first = column == 0
    last = column == width - 1

    def spread(x, ref, p, row):
        back = jnp.where(first, 0.0, pltpu.roll(x, 1, 0))
        ahead = jnp.where(last, 0.0, pltpu.roll(x, chunk - 1, 0))
        ref[p, pl.ds(row, chunk), :] = jnp.concatenate([back, x, ahead], axis=1).astype(BF16)

    def each(count, body):
        def step(k, carry):
            body(k // 4, pl.multiple_of(lax.rem(k, 4) * chunk, chunk))
            return carry

        lax.fori_loop(0, 4 * count, step, 0)

    def halo(kind, low_src, high_src, low_dst, high_dst):
        left = pltpu.make_async_remote_copy(
            low_src, high_dst, hs_sem.at[kind, 0], hr_sem.at[kind, 0],
            device_id={"space": lax.rem(me + n - 1, n)}, device_id_type=MESH,
        )
        right = pltpu.make_async_remote_copy(
            high_src, low_dst, hs_sem.at[kind, 1], hr_sem.at[kind, 1],
            device_id={"space": lax.rem(me + 1, n)}, device_id_type=MESH,
        )

        def start():
            @pl.when(me > 0)
            def _():
                left.start()

            @pl.when(me < n - 1)
            def _():
                right.start()

        def wait_recv():
            @pl.when(me < n - 1)
            def _():
                left.wait_recv()

            @pl.when(me == n - 1)
            def _():
                high_dst[...] = jnp.zeros(high_dst.shape, BF16)

            @pl.when(me > 0)
            def _():
                right.wait_recv()

            @pl.when(me == 0)
            def _():
                low_dst[...] = jnp.zeros(low_dst.shape, BF16)

        def wait_send():
            @pl.when(me > 0)
            def _():
                left.wait_send()

            @pl.when(me < n - 1)
            def _():
                right.wait_send()

        return start, wait_recv, wait_send

    end = (planes - 1) * plane
    volume_halo = halo(
        0, vs.at[0], vs.at[1], vh.at[0], vh.at[1]
    )
    cot_halo = halo(
        1, cot.at[pl.ds(0, plane)], cot.at[pl.ds(end, plane)],
        ct.at[0, pl.ds(width, plane)], ct.at[planes + 1, pl.ds(width, plane)],
    )
    act_halo = halo(
        2, sa.at[0], sa.at[1], ah.at[0], ah.at[1]
    )
    grad_halo = halo(
        3, gs.at[0], gs.at[1], gh.at[0], gh.at[1]
    )

    local[0].wait()

    def pack(raw, ref):
        for side, start in enumerate((0, end)):
            for k in range(2):
                low = raw[pl.ds(start + k * chunk, chunk), :].astype(F32)
                high = raw[pl.ds(start + (2 + k) * chunk, chunk), :].astype(F32)
                ref[side, pl.ds(k * chunk, chunk), :] = jnp.concatenate(
                    [low, high], axis=1
                ).astype(BF16)

    pack(vraw, vs)

    pl.semaphore_wait(barrier, n - 1)
    volume_halo[0]()
    cot_halo[0]()

    def own_volume(p, row):
        x = vraw[pl.ds(pl.multiple_of(p * plane + row, chunk), chunk), :].astype(F32)
        spread(x, pv, p + 1, row + width)

    each(planes, own_volume)

    def halo_planes(slots, ref):
        def body(k, carry):
            p, row = k // 2, pl.multiple_of(lax.rem(k, 2) * chunk, chunk)
            x = slots[p, pl.ds(row, chunk), :].astype(F32)
            half = x.shape[1] // 2
            spread(x[:, :half], ref, p * (planes + 1), row + width)
            spread(x[:, half:], ref, p * (planes + 1), row + width + 2 * chunk)
            return carry

        lax.fori_loop(0, 4, body, 0)

    def conv(ref, kernels, p, row, taps=(0, 1, 2), total=None):
        for a in taps:
            for b in range(3):
                term = jnp.dot(
                    ref[p + a, pl.ds(pl.multiple_of(row + b * width, width), chunk), :],
                    kernels[a * 3 + b],
                    preferred_element_type=F32,
                )
                total = term if total is None else total + term
        return total

    def parted(p):
        inner = [a for a in range(3) if 1 <= p + a <= planes]
        return inner, [a for a in range(3) if a not in inner]

    def chunks(body):
        def step(k, carry):
            body(pl.multiple_of(k * chunk, chunk))
            return carry

        lax.fori_loop(0, 4, step, 0)

    for p in range(planes):

        def inner_conv(row, p=p):
            at = pl.ds(pl.multiple_of(p * plane + row, chunk), chunk)
            dsl[at, :] = conv(pv, w1, p, row, parted(p)[0])

        chunks(inner_conv)

    volume_halo[1]()
    halo_planes(vh, pv)

    def first_conv(p, row):
        at = pl.ds(pl.multiple_of(p * plane + row, chunk), chunk)
        hidden = conv(pv, w1, p, row, parted(p)[1], dsl[at, :])
        s = jax.nn.sigmoid(hidden)
        dsl[at, :] = s * (1.0 + hidden * (1.0 - s))
        rounded = (hidden * s).astype(BF16)
        araw[at, :] = rounded
        spread(rounded.astype(F32), pa, p + 1, row + width)

    for p in range(planes):
        chunks(functools.partial(first_conv, p))
    pack(araw, sa)
    act_halo[0]()

    for copy in local[1:]:
        copy.wait()
    cot_halo[1]()
    low_lanes = lax.broadcasted_iota(jnp.int32, (1, 2 * cm), 1) < cm

    def back_conv(p, row):
        pieces = [
            ct[p + a, pl.ds(pl.multiple_of(row + b * width, width), chunk), :]
            for a in range(3)
            for b in range(3)
        ]
        y = jnp.dot(jnp.concatenate(pieces, axis=1), wg[...], preferred_element_type=F32)
        z = y[:, : 2 * cm]
        z = jnp.where(
            low_lanes,
            jnp.where(first, 0.0, pltpu.roll(z, 1, 0)),
            jnp.where(last, 0.0, pltpu.roll(z, chunk - 1, 0)),
        )
        grad_act = z[:, :cm] + z[:, cm:] + y[:, 2 * cm :]
        at = pl.ds(pl.multiple_of(p * plane + row, chunk), chunk)
        rounded = (grad_act * dsl[at, :]).astype(BF16)
        graw[at, :] = rounded
        spread(rounded.astype(F32), pg, p + 1, row + width)

    each(planes, back_conv)
    pack(graw, gs)
    grad_halo[0]()

    act_halo[1]()
    halo_planes(ah, pa)

    acc1[...] = jnp.zeros(acc1.shape, F32)
    acc2[...] = jnp.zeros(acc2.shape, F32)

    def kernel_terms(p, row):
        at = pl.ds(pl.multiple_of(p * plane + row, chunk), chunk)
        field2 = ct[p + 1, pl.ds(pl.multiple_of(row + width, width), chunk), :].T
        field1 = graw[at, :].T
        for a in range(3):
            for b in range(3):
                rows = pl.ds(pl.multiple_of(row + b * width, width), chunk)
                acc2[a * 3 + b] += jnp.dot(field2, pa[p + a, rows, :], preferred_element_type=F32)
                acc1[a * 3 + b] += jnp.dot(field1, pv[p + a, rows, :], preferred_element_type=F32)

    each(planes, kernel_terms)

    parity = lax.rem(me, 2)
    mine = me // 2
    used = 14 * (r1 + r2)
    for d in range(n):
        pieces = []
        for acc, r in ((acc2, r2), (acc1, r1)):
            taps = [acc[t, pl.ds(d * r, r), :] for t in range(9)]
            pieces += [x[:, : 2 * ci] for x in taps]
            last_taps = [x[:, 2 * ci :] for x in taps] + [jnp.zeros((r, ci), F32)]
            pieces += [
                jnp.concatenate(last_taps[2 * k : 2 * k + 2], axis=1) for k in range(5)
            ]
        if tx.shape[2] > used:
            pieces.append(jnp.zeros((tx.shape[2] - used, 2 * ci), F32))
        whole = jnp.concatenate(pieces, axis=0)
        own[d % 2, d // 2] = whole
        tx[d % 2, d // 2] = whole.astype(BF16)

    pair = pltpu.make_async_remote_copy(
        tx.at[1 - parity], rx, ps_sem.at[0], pr_sem.at[0],
        device_id={"space": me + 1 - 2 * parity}, device_id_type=MESH,
    )
    pair.start()

    def second_conv(p, row):
        at = pl.ds(pl.multiple_of(p * plane + row, chunk), chunk)
        out[at, :] = conv(pa, w2, p, row)

    each(1, second_conv)

    pair.wait_recv()

    def pair_sum(m, carry):
        ty[m] = (own[parity, m] + rx[m].astype(F32)).astype(BF16)
        return carry

    lax.fori_loop(0, n // 2, pair_sum, 0)
    sends = []
    for j in range(1, n // 2):
        slot = lax.rem(mine + j, n // 2)
        sends.append(
            pltpu.make_async_remote_copy(
                ty.at[slot], ry.at[j], ts_sem.at[j], tr_sem.at[j],
                device_id={"space": 2 * slot + parity}, device_id_type=MESH,
            )
        )
        sends[-1].start()

    def rest_second(p, row):
        second_conv(p + 1, row)

    each(planes - 1, rest_second)

    grad_halo[1]()
    halo_planes(gh, pg)

    def last_conv(p, row):
        at = pl.ds(pl.multiple_of(p * plane + row, chunk), chunk)
        gvol[at, :] = conv(pg, w1f, p, row)

    each(planes, last_conv)

    for send in sends:
        send.wait_recv()
    total = own[parity, mine] + rx[mine].astype(F32)
    for j in range(1, n // 2):
        total = total + ry[j].astype(F32)
    total = total * scale
    for t in range(14):
        taps = (3 * t, 3 * t + 1) if t < 9 else (6 * (t - 9) + 2, 6 * (t - 9) + 5)
        for half, tap in enumerate(taps):
            if tap < 27:
                lanes = slice(half * ci, (half + 1) * ci)
                g2[tap] = total[t * r2 : (t + 1) * r2, lanes]
                g1[tap] = total[14 * r2 + t * r1 : 14 * r2 + (t + 1) * r1, lanes]

    pair.wait_send()
    for send in sends:
        send.wait_send()
    for exchange in (volume_halo, cot_halo, act_halo, grad_halo):
        exchange[2]()


def shards(volume, weight_one, weight_two, cotangent):
    n = lax.axis_size("space")
    planes, height, width, ci = volume.shape
    cm, co = weight_two.shape[3], weight_two.shape[4]
    plane = height * width
    cells = planes * plane
    pad = plane + 2 * width
    scale = 1.0 / math.sqrt(cells * n)

    w1 = weight_one.reshape(9, 3 * ci, cm)
    w2 = weight_two.reshape(9, 3 * cm, co)

    vmem = pl.BlockSpec(memory_space=pltpu.VMEM)
    hbm = pl.BlockSpec(memory_space=pl.ANY)
    rows = -(-14 * (cm // n + co // n) // 16) * 16
    out, gvol, g1, g2 = pl.pallas_call(
        functools.partial(kernel, n, planes, height, width, ci, cm, co, scale),
        out_shape=(
            jax.ShapeDtypeStruct((cells, co), F32),
            jax.ShapeDtypeStruct((cells, ci), F32),
            jax.ShapeDtypeStruct((27, cm // n, ci), F32),
            jax.ShapeDtypeStruct((27, co // n, cm), F32),
        ),
        in_specs=[hbm, hbm, vmem, vmem],
        out_specs=(vmem, vmem, vmem, vmem),
        scratch_shapes=[
            pltpu.VMEM((planes + 2, pad, 3 * ci), BF16),
            pltpu.VMEM((planes + 2, pad, 3 * cm), BF16),
            pltpu.VMEM((planes + 2, pad, 3 * cm), BF16),
            pltpu.VMEM((planes + 2, pad, co), BF16),
            pltpu.VMEM((cells, ci), BF16),
            pltpu.VMEM((cells, cm), BF16),
            pltpu.VMEM((cells, cm), BF16),
            pltpu.VMEM((2, plane // 2, 2 * ci), BF16),
            pltpu.VMEM((2, plane // 2, 2 * cm), BF16),
            pltpu.VMEM((2, plane // 2, 2 * cm), BF16),
            pltpu.VMEM((2, plane // 2, 2 * ci), BF16),
            pltpu.VMEM((2, plane // 2, 2 * cm), BF16),
            pltpu.VMEM((2, plane // 2, 2 * cm), BF16),
            pltpu.VMEM((cells, cm), F32),
            pltpu.VMEM((9, cm, 3 * ci), F32),
            pltpu.VMEM((9, co, 3 * cm), F32),
            pltpu.VMEM((9, 3 * cm, ci), BF16),
            pltpu.VMEM((9 * co, 3 * cm), BF16),
            pltpu.VMEM((2, n // 2, rows, 2 * ci), F32),
            pltpu.VMEM((2, n // 2, rows, 2 * ci), BF16),
            pltpu.VMEM((n // 2, rows, 2 * ci), BF16),
            pltpu.VMEM((n // 2, rows, 2 * ci), BF16),
            pltpu.VMEM((n // 2, rows, 2 * ci), BF16),
            pltpu.SemaphoreType.DMA((1 + planes,)),
            pltpu.SemaphoreType.DMA((4, 2)),
            pltpu.SemaphoreType.DMA((4, 2)),
            pltpu.SemaphoreType.DMA((1,)),
            pltpu.SemaphoreType.DMA((1,)),
            pltpu.SemaphoreType.DMA((n // 2,)),
            pltpu.SemaphoreType.DMA((n // 2,)),
        ],
        compiler_params=pltpu.CompilerParams(
            collective_id=0, has_side_effects=True, vmem_limit_bytes=38 << 20
        ),
    )(
        volume.reshape(cells, ci), cotangent.reshape(cells, co), w1, w2
    )
    return (
        out.reshape(planes, height, width, co),
        gvol.reshape(planes, height, width, ci),
        jnp.transpose(g1.reshape(3, 3, 3, cm // n, ci), (0, 1, 2, 4, 3)),
        jnp.transpose(g2.reshape(3, 3, 3, co // n, cm), (0, 1, 2, 4, 3)),
    )


def solution(mesh):
    return jax.shard_map(
        shards,
        mesh=mesh,
        in_specs=(
            P(("groups", "space"), None, None, None),
            P(),
            P(),
            P(("groups", "space"), None, None, None),
        ),
        out_specs=(
            P(("groups", "space"), None, None, None),
            P(("groups", "space"), None, None, None),
            P("groups", None, None, None, "space"),
            P("groups", None, None, None, "space"),
        ),
        check_vma=False,
    )
```

```python
import functools
import math

import jax
import jax.numpy as jnp
from jax import lax
from jax.experimental import pallas as pl
from jax.experimental.pallas import tpu as pltpu
from jax.sharding import PartitionSpec as P

MESH = pl.DeviceIdType.MESH
F32 = jnp.float32
BF16 = jnp.bfloat16
TN = (((0,), (0,)), ((), ()))


def kernel(
    n, planes, height, width, ci, cm, co, scale,
    vol, cot, w1_in, w2_in,
    out_hbm, gvol_hbm, g1, g2,
    out, gvol, pv, pa, pg, ct, vraw, araw, graw, vs, sa, gs, vh, ah, gh, dsl, acc1, acc2,
    w1, w2, w1f, wg, own, tx, rx, ty, ry,
    loc_sem, st_sem, hs_sem, hr_sem, ps_sem, pr_sem, ts_sem, tr_sem,
):
    me = lax.axis_index("space")
    plane = height * width
    chunk = plane // 4
    pad = plane + 2 * width
    r1, r2 = cm // n, co // n

    barrier = pltpu.get_barrier_semaphore()
    for j in range(1, n):
        pl.semaphore_signal(
            barrier, inc=1, device_id={"space": lax.rem(me + j, n)}, device_id_type=MESH
        )

    local = [pltpu.make_async_copy(vol, vraw, loc_sem.at[0])]
    for p in range(planes):
        local.append(
            pltpu.make_async_copy(
                cot.at[pl.ds(p * plane, plane)],
                ct.at[p + 1, pl.ds(width, plane)],
                loc_sem.at[1 + p],
            )
        )
    weights = [
        pltpu.make_async_copy(w2_in, w2, loc_sem.at[1 + planes]),
        pltpu.make_async_copy(w1_in, w1, loc_sem.at[2 + planes]),
    ]
    for copy in local[:1] + weights + local[1:]:
        copy.start()

    for copy in weights:
        copy.wait()

    for t in range(9):
        w = w2[8 - t]
        order = [w[2 * cm :], w[:cm], w[cm : 2 * cm]]
        wg[pl.ds(t * co, co), :] = jnp.concatenate(order, axis=0).T
        w = w1[8 - t]
        for c in range(3):
            w1f[t, pl.ds(c * cm, cm), :] = w[(2 - c) * ci : (3 - c) * ci].T

    for ref in (pv, pa, pg, ct):
        zero = jnp.zeros((width, ref.shape[2]), BF16)
        for p in range(planes + 2):
            ref[p, pl.ds(0, width), :] = zero
            ref[p, pl.ds(pad - width, width), :] = zero

    column = lax.broadcasted_iota(jnp.int32, (chunk, 1), 0) % width
    first = column == 0
    last = column == width - 1

    def spread(x, ref, p, row):
        back = jnp.where(first, 0.0, pltpu.roll(x, 1, 0))
        ahead = jnp.where(last, 0.0, pltpu.roll(x, chunk - 1, 0))
        ref[p, pl.ds(row, chunk), :] = jnp.concatenate([back, x, ahead], axis=1).astype(BF16)

    def each(count, body):
        def step(k, carry):
            body(k // 4, pl.multiple_of(lax.rem(k, 4) * chunk, chunk))
            return carry

        lax.fori_loop(0, 4 * count, step, 0)

    def halo(kind, low_src, high_src, low_dst, high_dst):
        left = pltpu.make_async_remote_copy(
            low_src, high_dst, hs_sem.at[kind, 0], hr_sem.at[kind, 0],
            device_id={"space": lax.rem(me + n - 1, n)}, device_id_type=MESH,
        )
        right = pltpu.make_async_remote_copy(
            high_src, low_dst, hs_sem.at[kind, 1], hr_sem.at[kind, 1],
            device_id={"space": lax.rem(me + 1, n)}, device_id_type=MESH,
        )

        def start():
            @pl.when(me > 0)
            def _():
                left.start()

            @pl.when(me < n - 1)
            def _():
                right.start()

        def wait_recv():
            @pl.when(me < n - 1)
            def _():
                left.wait_recv()

            @pl.when(me == n - 1)
            def _():
                high_dst[...] = jnp.zeros(high_dst.shape, BF16)

            @pl.when(me > 0)
            def _():
                right.wait_recv()

            @pl.when(me == 0)
            def _():
                low_dst[...] = jnp.zeros(low_dst.shape, BF16)

        def wait_send():
            @pl.when(me > 0)
            def _():
                left.wait_send()

            @pl.when(me < n - 1)
            def _():
                right.wait_send()

        return start, wait_recv, wait_send

    end = (planes - 1) * plane
    volume_halo = halo(
        0, vs.at[0], vs.at[1], vh.at[0], vh.at[1]
    )
    cot_halo = halo(
        1, cot.at[pl.ds(0, plane)], cot.at[pl.ds(end, plane)],
        ct.at[0, pl.ds(width, plane)], ct.at[planes + 1, pl.ds(width, plane)],
    )
    act_halo = halo(
        2, sa.at[0], sa.at[1], ah.at[0], ah.at[1]
    )
    grad_halo = halo(
        3, gs.at[0], gs.at[1], gh.at[0], gh.at[1]
    )

    local[0].wait()

    def pack(raw, ref):
        for side, start in enumerate((0, end)):
            for k in range(2):
                low = raw[pl.ds(start + k * chunk, chunk), :].astype(F32)
                high = raw[pl.ds(start + (2 + k) * chunk, chunk), :].astype(F32)
                ref[side, pl.ds(k * chunk, chunk), :] = jnp.concatenate(
                    [low, high], axis=1
                ).astype(BF16)

    pack(vraw, vs)

    pl.semaphore_wait(barrier, n - 1)
    volume_halo[0]()
    cot_halo[0]()

    def own_volume(p, row):
        x = vraw[pl.ds(pl.multiple_of(p * plane + row, chunk), chunk), :].astype(F32)
        spread(x, pv, p + 1, row + width)

    each(planes, own_volume)

    def halo_planes(slots, ref):
        def body(k, carry):
            p, row = k // 2, pl.multiple_of(lax.rem(k, 2) * chunk, chunk)
            x = slots[p, pl.ds(row, chunk), :].astype(F32)
            half = x.shape[1] // 2
            spread(x[:, :half], ref, p * (planes + 1), row + width)
            spread(x[:, half:], ref, p * (planes + 1), row + width + 2 * chunk)
            return carry

        lax.fori_loop(0, 4, body, 0)

    def conv(ref, kernels, p, row, taps=(0, 1, 2), total=None):
        for a in taps:
            for b in range(3):
                term = jnp.dot(
                    ref[p + a, pl.ds(pl.multiple_of(row + b * width, width), chunk), :],
                    kernels[a * 3 + b],
                    preferred_element_type=F32,
                )
                total = term if total is None else total + term
        return total

    def parted(p):
        inner = [a for a in range(3) if 1 <= p + a <= planes]
        return inner, [a for a in range(3) if a not in inner]

    def chunks(body):
        def step(k, carry):
            body(pl.multiple_of(k * chunk, chunk))
            return carry

        lax.fori_loop(0, 4, step, 0)

    for p in range(planes):

        def inner_conv(row, p=p):
            at = pl.ds(pl.multiple_of(p * plane + row, chunk), chunk)
            dsl[at, :] = conv(pv, w1, p, row, parted(p)[0])

        chunks(inner_conv)

    volume_halo[1]()
    halo_planes(vh, pv)

    def first_conv(p, row):
        at = pl.ds(pl.multiple_of(p * plane + row, chunk), chunk)
        hidden = conv(pv, w1, p, row, parted(p)[1], dsl[at, :])
        s = jax.nn.sigmoid(hidden)
        dsl[at, :] = s * (1.0 + hidden * (1.0 - s))
        rounded = (hidden * s).astype(BF16)
        araw[at, :] = rounded
        spread(rounded.astype(F32), pa, p + 1, row + width)

    for p in range(planes):
        chunks(functools.partial(first_conv, p))
    pack(araw, sa)
    act_halo[0]()

    for copy in local[1:]:
        copy.wait()
    cot_halo[1]()
    low_lanes = lax.broadcasted_iota(jnp.int32, (1, 2 * cm), 1) < cm

    def back_conv(p, row):
        pieces = [
            ct[p + a, pl.ds(pl.multiple_of(row + b * width, width), chunk), :]
            for a in range(3)
            for b in range(3)
        ]
        y = jnp.dot(jnp.concatenate(pieces, axis=1), wg[...], preferred_element_type=F32)
        z = y[:, : 2 * cm]
        z = jnp.where(
            low_lanes,
            jnp.where(first, 0.0, pltpu.roll(z, 1, 0)),
            jnp.where(last, 0.0, pltpu.roll(z, chunk - 1, 0)),
        )
        grad_act = z[:, :cm] + z[:, cm:] + y[:, 2 * cm :]
        at = pl.ds(pl.multiple_of(p * plane + row, chunk), chunk)
        rounded = (grad_act * dsl[at, :]).astype(BF16)
        graw[at, :] = rounded
        spread(rounded.astype(F32), pg, p + 1, row + width)

    each(planes, back_conv)
    pack(graw, gs)
    grad_halo[0]()

    act_halo[1]()
    halo_planes(ah, pa)

    acc1[...] = jnp.zeros(acc1.shape, F32)
    acc2[...] = jnp.zeros(acc2.shape, F32)

    def kernel_terms(p, row):
        at = pl.ds(pl.multiple_of(p * plane + row, chunk), chunk)
        field2 = ct[p + 1, pl.ds(pl.multiple_of(row + width, width), chunk), :].T
        field1 = graw[at, :].T
        for a in range(3):
            for b in range(3):
                rows = pl.ds(pl.multiple_of(row + b * width, width), chunk)
                acc2[a * 3 + b] += jnp.dot(field2, pa[p + a, rows, :], preferred_element_type=F32)
                acc1[a * 3 + b] += jnp.dot(field1, pv[p + a, rows, :], preferred_element_type=F32)

    each(planes, kernel_terms)

    parity = lax.rem(me, 2)
    mine = me // 2
    used = 14 * (r1 + r2)
    for d in range(n):
        pieces = []
        for acc, r in ((acc2, r2), (acc1, r1)):
            taps = [acc[t, pl.ds(d * r, r), :] for t in range(9)]
            pieces += [x[:, : 2 * ci] for x in taps]
            last_taps = [x[:, 2 * ci :] for x in taps] + [jnp.zeros((r, ci), F32)]
            pieces += [
                jnp.concatenate(last_taps[2 * k : 2 * k + 2], axis=1) for k in range(5)
            ]
        if tx.shape[2] > used:
            pieces.append(jnp.zeros((tx.shape[2] - used, 2 * ci), F32))
        whole = jnp.concatenate(pieces, axis=0)
        own[d % 2, d // 2] = whole
        tx[d % 2, d // 2] = whole.astype(BF16)

    pair = pltpu.make_async_remote_copy(
        tx.at[1 - parity], rx, ps_sem.at[0], pr_sem.at[0],
        device_id={"space": me + 1 - 2 * parity}, device_id_type=MESH,
    )
    pair.start()

    def second_conv(p, row):
        at = pl.ds(pl.multiple_of(p * plane + row, chunk), chunk)
        out[at, :] = conv(pa, w2, p, row)

    each(1, second_conv)
    stores = [
        pltpu.make_async_copy(
            out.at[pl.ds(lo, size)], out_hbm.at[pl.ds(lo, size)], st_sem.at[k]
        )
        for k, (lo, size) in enumerate(((0, plane), (plane, (planes - 1) * plane)))
    ]
    stores.append(pltpu.make_async_copy(gvol, gvol_hbm, st_sem.at[2]))
    stores[0].start()

    pair.wait_recv()

    def pair_sum(m, carry):
        ty[m] = (own[parity, m] + rx[m].astype(F32)).astype(BF16)
        return carry

    lax.fori_loop(0, n // 2, pair_sum, 0)
    sends = []
    for j in range(1, n // 2):
        slot = lax.rem(mine + j, n // 2)
        sends.append(
            pltpu.make_async_remote_copy(
                ty.at[slot], ry.at[j], ts_sem.at[j], tr_sem.at[j],
                device_id={"space": 2 * slot + parity}, device_id_type=MESH,
            )
        )
        sends[-1].start()

    def rest_second(p, row):
        second_conv(p + 1, row)

    each(planes - 1, rest_second)
    stores[1].start()

    grad_halo[1]()
    halo_planes(gh, pg)

    def last_conv(p, row):
        at = pl.ds(pl.multiple_of(p * plane + row, chunk), chunk)
        gvol[at, :] = conv(pg, w1f, p, row)

    each(planes, last_conv)
    stores[2].start()

    for send in sends:
        send.wait_recv()
    total = own[parity, mine] + rx[mine].astype(F32)
    for j in range(1, n // 2):
        total = total + ry[j].astype(F32)
    total = total * scale
    for t in range(14):
        taps = (3 * t, 3 * t + 1) if t < 9 else (6 * (t - 9) + 2, 6 * (t - 9) + 5)
        for half, tap in enumerate(taps):
            if tap < 27:
                lanes = slice(half * ci, (half + 1) * ci)
                g2[tap] = total[t * r2 : (t + 1) * r2, lanes]
                g1[tap] = total[14 * r2 + t * r1 : 14 * r2 + (t + 1) * r1, lanes]

    for store in stores:
        store.wait()
    pair.wait_send()
    for send in sends:
        send.wait_send()
    for exchange in (volume_halo, cot_halo, act_halo, grad_halo):
        exchange[2]()


def shards(volume, weight_one, weight_two, cotangent):
    n = lax.axis_size("space")
    planes, height, width, ci = volume.shape
    cm, co = weight_two.shape[3], weight_two.shape[4]
    plane = height * width
    cells = planes * plane
    pad = plane + 2 * width
    scale = 1.0 / math.sqrt(cells * n)

    w1 = weight_one.reshape(9, 3 * ci, cm)
    w2 = weight_two.reshape(9, 3 * cm, co)

    vmem = pl.BlockSpec(memory_space=pltpu.VMEM)
    hbm = pl.BlockSpec(memory_space=pltpu.HBM)
    rows = -(-14 * (cm // n + co // n) // 16) * 16
    out, gvol, g1, g2 = pl.pallas_call(
        functools.partial(kernel, n, planes, height, width, ci, cm, co, scale),
        out_shape=(
            jax.ShapeDtypeStruct((cells, co), F32),
            jax.ShapeDtypeStruct((cells, ci), F32),
            jax.ShapeDtypeStruct((27, cm // n, ci), F32),
            jax.ShapeDtypeStruct((27, co // n, cm), F32),
        ),
        in_specs=[hbm, hbm, hbm, hbm],
        out_specs=(hbm, hbm, vmem, vmem),
        scratch_shapes=[
            pltpu.VMEM((cells, co), F32),
            pltpu.VMEM((cells, ci), F32),
            pltpu.VMEM((planes + 2, pad, 3 * ci), BF16),
            pltpu.VMEM((planes + 2, pad, 3 * cm), BF16),
            pltpu.VMEM((planes + 2, pad, 3 * cm), BF16),
            pltpu.VMEM((planes + 2, pad, co), BF16),
            pltpu.VMEM((cells, ci), BF16),
            pltpu.VMEM((cells, cm), BF16),
            pltpu.VMEM((cells, cm), BF16),
            pltpu.VMEM((2, plane // 2, 2 * ci), BF16),
            pltpu.VMEM((2, plane // 2, 2 * cm), BF16),
            pltpu.VMEM((2, plane // 2, 2 * cm), BF16),
            pltpu.VMEM((2, plane // 2, 2 * ci), BF16),
            pltpu.VMEM((2, plane // 2, 2 * cm), BF16),
            pltpu.VMEM((2, plane // 2, 2 * cm), BF16),
            pltpu.VMEM((cells, cm), F32),
            pltpu.VMEM((9, cm, 3 * ci), F32),
            pltpu.VMEM((9, co, 3 * cm), F32),
            pltpu.VMEM((9, 3 * ci, cm), BF16),
            pltpu.VMEM((9, 3 * cm, co), BF16),
            pltpu.VMEM((9, 3 * cm, ci), BF16),
            pltpu.VMEM((9 * co, 3 * cm), BF16),
            pltpu.VMEM((2, n // 2, rows, 2 * ci), F32),
            pltpu.VMEM((2, n // 2, rows, 2 * ci), BF16),
            pltpu.VMEM((n // 2, rows, 2 * ci), BF16),
            pltpu.VMEM((n // 2, rows, 2 * ci), BF16),
            pltpu.VMEM((n // 2, rows, 2 * ci), BF16),
            pltpu.SemaphoreType.DMA((3 + planes,)),
            pltpu.SemaphoreType.DMA((3,)),
            pltpu.SemaphoreType.DMA((4, 2)),
            pltpu.SemaphoreType.DMA((4, 2)),
            pltpu.SemaphoreType.DMA((1,)),
            pltpu.SemaphoreType.DMA((1,)),
            pltpu.SemaphoreType.DMA((n // 2,)),
            pltpu.SemaphoreType.DMA((n // 2,)),
        ],
        compiler_params=pltpu.CompilerParams(
            collective_id=0, has_side_effects=True, vmem_limit_bytes=60 << 20
        ),
    )(
        volume.reshape(cells, ci), cotangent.reshape(cells, co), w1, w2
    )
    return (
        out.reshape(planes, height, width, co),
        gvol.reshape(planes, height, width, ci),
        jnp.transpose(g1.reshape(3, 3, 3, cm // n, ci), (0, 1, 2, 4, 3)),
        jnp.transpose(g2.reshape(3, 3, 3, co // n, cm), (0, 1, 2, 4, 3)),
    )


def solution(mesh):
    return jax.shard_map(
        shards,
        mesh=mesh,
        in_specs=(
            P(("groups", "space"), None, None, None),
            P(),
            P(),
            P(("groups", "space"), None, None, None),
        ),
        out_specs=(
            P(("groups", "space"), None, None, None),
            P(("groups", "space"), None, None, None),
            P("groups", None, None, None, "space"),
            P("groups", None, None, None, "space"),
        ),
        check_vma=False,
    )
```
